32 devices in a mesh: seq: 16 (over z, y, core), head: 2 (over x).
Axes of the slice: x: 2, y: 2, z: 4, core: 2. Of those that a mesh axis runs over, the one named last changes fastest.
Arguments:
- queries: bfloat16 [4096, 768], P('seq', 'head'), may hold values from -37 to 37
- key_rows: bfloat16 [4096, 768], P('seq', 'head'), may hold values from -4 to 4
- value_rows: bfloat16 [4096, 768], P('seq', 'head'), may hold values from -5 to 5
- out_grad: bfloat16 [4096, 768], P('seq', 'head'), may hold values from -80 to 80
- query_weight: bfloat16 [5120, 768], P('seq', 'head'), may hold values from -0.078125 to 0.078125
- neighbour_tiles: int32 [32, 12], replicated, may hold values from 0 to 31, as said below
- neighbour_count: int32 [32], replicated, may hold values from 1 to 12, as said below
Outputs:
- input_grad: bfloat16 [4096, 5120], P('seq', 'head')
- key_grad: bfloat16 [4096, 768], P('seq', 'head')
- value_grad: bfloat16 [4096, 768], P('seq', 'head')
The draws below stay inside these ranges and needn't reach their ends.
Inputs may be any that keep to these rules, and one draw needn't show every extreme that they name: `neighbour_tiles`: the first neighbour_count[g] entries of row g are distinct tiles of frames t - 1, t and t + 1, where t is tile g's frame, at most one row and one column away from g, and include g itself; the remaining entries repeat g. `neighbour_count`: some tile has 12 live entries.
All inputs are finite; a program needn't handle non-finite values.
Results may differ from the reference program's by a relative error of at most 0.012.
Values may be sent and summed in bfloat16 or wider, within the bound.
No kernel may reach another device: no remote copies, remote signals or barrier semaphores. Data moves between devices by JAX's collectives and lax.ppermute only.
A program may use at most 64 MiB of HBM per device.

```python
import jax
import jax.numpy as jnp
from jax import lax

D = 5120
HEAD_DIM = 128
TILE = 128
TH = 2
TW = 2
TILES_DEV = 2
MAXN = 12
REACH = 4
TOKENS = 4096
NTILES = 32
HEADS = 6
N_SEQ = 16
N_HEAD = 2


def query_key_pair(key):
    base = jax.random.fold_in(key, 31)
    query_key, keys_key = jax.random.split(base)
    width = HEADS * HEAD_DIM
    keys_f = jnp.clip(jax.random.normal(keys_key, (TOKENS, width), jnp.float32), -4.0, 4.0)
    query_f = jnp.clip(jax.random.normal(query_key, (TOKENS, width), jnp.float32), -4.0, 4.0)
    return (query_f.astype(jnp.bfloat16), keys_f.astype(jnp.bfloat16))


def draw_queries(key, part):
    return query_key_pair(key)[0]


def draw_key_rows(key, part):
    return query_key_pair(key)[1]


def tile_lists(key):
    base = jax.random.fold_in(key, 101)
    rate_key, coin_key, full_key = jax.random.split(base, 3)
    frame_key, height_key, across_key = jax.random.split(full_key, 3)
    frame_tiles = TH * TW
    frames = NTILES // frame_tiles
    keep_rate = jax.random.randint(rate_key, (frames,), 25, 101)
    tiles = jnp.arange(NTILES, dtype=jnp.int32)
    frame = tiles // frame_tiles
    height = tiles // TW % TH
    across = tiles % TW
    offsets = jnp.array([[a, b, c] for a in (-1, 0, 1) for b in (-1, 0, 1) for c in (-1, 0, 1)], jnp.int32)
    cand_frame = frame[:, None] + offsets[None, :, 0]
    cand_height = height[:, None] + offsets[None, :, 1]
    cand_across = across[:, None] + offsets[None, :, 2]
    valid = (cand_frame >= 0) & (cand_frame < frames) & (cand_height >= 0) & (cand_height < TH) & (cand_across >= 0) & (cand_across < TW)
    target = (cand_frame * TH + cand_height) * TW + cand_across
    coins = jax.random.randint(coin_key, (NTILES, 27), 0, 100)
    centre = (offsets[:, 0] == 0) & (offsets[:, 1] == 0) & (offsets[:, 2] == 0)
    height_lo = 1 if TH >= 3 else 0
    height_hi = TH - 1 if TH >= 3 else TH
    across_lo = 1 if TW >= 3 else 0
    across_hi = TW - 1 if TW >= 3 else TW
    full_frame = jax.random.randint(frame_key, (), 1, frames - 1)
    full_height = jax.random.randint(height_key, (), height_lo, height_hi)
    full_across = jax.random.randint(across_key, (), across_lo, across_hi)
    full_tile = (full_frame * TH + full_height) * TW + full_across
    chosen = (coins < keep_rate[frame][:, None]) | centre[None, :] | (tiles == full_tile)[:, None]
    keep = valid & chosen
    ranking = (1 - keep.astype(jnp.int32)) * 64 + jnp.arange(27, dtype=jnp.int32)[None, :]
    order = jnp.argsort(ranking, axis=1)
    target_sorted = jnp.take_along_axis(target, order, axis=1)[:, :MAXN]
    keep_sorted = jnp.take_along_axis(keep, order, axis=1)[:, :MAXN]
    lists = jnp.where(keep_sorted, target_sorted, tiles[:, None]).astype(jnp.int32)
    counts = jnp.sum(keep.astype(jnp.int32), axis=1).astype(jnp.int32)
    return (lists, counts)


def draw_neighbour_tiles(key, part):
    return tile_lists(key)[0]


def draw_neighbour_count(key, part):
    return tile_lists(key)[1]


def levels(key, shape, pieces, least, top_value):
    level = 1.0
    for axis_at, blocks in pieces:
        draws = jax.random.uniform(jax.random.fold_in(jax.random.fold_in(key, 6), axis_at), (blocks,), jnp.float32, least / len(pieces), top_value / len(pieces))
        level = level * jnp.repeat(jnp.exp(draws), shape[axis_at] // blocks).reshape((-1,) + (1,) * (len(shape) - 1 - axis_at))
    return level


def normal_values(stream_key, shape, scale, reach, shards=(), held_as=jnp.bfloat16):
    values = scale * jax.random.normal(stream_key, shape, jnp.float32)
    if shards:
        values = values * levels(stream_key, shape, shards, -0.22, 0.18)
    return jnp.clip(values, -reach, reach).astype(held_as)


def setup_inputs(seed: int = 0) -> dict:
    key_list = jax.random.split(jax.random.key(seed), 8)
    queries = draw_queries(jax.random.fold_in(key_list[7], 71), 0)
    key_rows = draw_key_rows(jax.random.fold_in(key_list[7], 71), 0)
    value_rows = normal_values(key_list[2], (TOKENS, HEADS * HEAD_DIM), 1.0, 5.0, ((0, 16), (1, 2)))
    out_grad = normal_values(key_list[3], (TOKENS, HEADS * HEAD_DIM), 16.0, 80.0, ((0, 16), (1, 2)))
    query_weight = normal_values(key_list[4], (D, HEADS * HEAD_DIM), D ** -0.5, 0.078125, ((0, 16), (1, 2)))
    neighbour_tiles = draw_neighbour_tiles(jax.random.fold_in(key_list[7], 71), 0)
    neighbour_count = draw_neighbour_count(jax.random.fold_in(key_list[7], 71), 0)
    return {"queries": queries, "key_rows": key_rows, "value_rows": value_rows, "out_grad": out_grad, "query_weight": query_weight, "neighbour_tiles": neighbour_tiles, "neighbour_count": neighbour_count}


def live_tiles(lists, counts, targets):
    slots = jnp.arange(lists.shape[1], dtype=jnp.int32)
    used = slots[None, :] < counts[:, None]
    hits = (lists[:, :, None] == targets[None, None, :]) & used[:, :, None]
    return jnp.any(hits, axis=1)


def expand_rows(mask, tile):
    return jnp.repeat(jnp.repeat(mask, tile, axis=0), tile, axis=1)


def padded_lists(tiles, counts, margin):
    edge = jnp.full((margin, tiles.shape[1]), -1, jnp.int32)
    lists = jnp.concatenate([edge, tiles, edge], axis=0)
    blank = jnp.zeros((margin,), jnp.int32)
    return lists, jnp.concatenate([blank, counts, blank], axis=0)


def low_round(values):
    return lax.optimization_barrier(values.astype(jnp.bfloat16)).astype(jnp.float32)


def reference(queries, key_rows, value_rows, out_grad, query_weight, neighbour_tiles, neighbour_count):
    softmax_scale = HEAD_DIM ** -0.5
    shard_rows = TILES_DEV * TILE
    margin = REACH * TILES_DEV
    window_tiles = (2 * REACH + 1) * TILES_DEV
    window_rows = window_tiles * TILE
    width = HEADS * HEAD_DIM
    pad_rows = margin * TILE
    blank_rows = jnp.zeros((pad_rows, width), jnp.bfloat16)
    keys_padded = jnp.concatenate([blank_rows, key_rows, blank_rows], axis=0)
    values_padded = jnp.concatenate([blank_rows, value_rows, blank_rows], axis=0)
    lists, counts = padded_lists(neighbour_tiles, neighbour_count, margin)

    def one_shard(carry, position):
        first_tile = position * TILES_DEV
        first_row = position * shard_rows
        query_block = lax.dynamic_slice_in_dim(queries, first_row, shard_rows, 0).astype(jnp.float32).reshape(shard_rows, HEADS, HEAD_DIM)
        grad_block = lax.dynamic_slice_in_dim(out_grad, first_row, shard_rows, 0).astype(jnp.float32).reshape(shard_rows, HEADS, HEAD_DIM)
        key_window = lax.dynamic_slice_in_dim(keys_padded, first_row, window_rows, 0).astype(jnp.float32).reshape(window_rows, HEADS, HEAD_DIM)
        value_window = lax.dynamic_slice_in_dim(values_padded, first_row, window_rows, 0).astype(jnp.float32).reshape(window_rows, HEADS, HEAD_DIM)
        own_lists = lax.dynamic_slice_in_dim(lists, first_tile + margin, TILES_DEV, 0)
        own_counts = lax.dynamic_slice_in_dim(counts, first_tile + margin, TILES_DEV, 0)
        targets = first_tile - margin + jnp.arange(window_tiles, dtype=jnp.int32)
        mask = expand_rows(live_tiles(own_lists, own_counts, targets), TILE)
        scores = jnp.einsum("qhd,khd->hqk", query_block, key_window) * softmax_scale
        masked = jnp.where(mask[None], scores, -jnp.inf)
        row_max = jnp.max(masked, axis=2, keepdims=True)
        row_sum = jnp.sum(jnp.exp(masked - row_max), axis=2, keepdims=True)
        log_norm = row_max + jnp.log(row_sum)
        probs = jnp.exp(masked - log_norm)
        probs_low = low_round(probs)
        attended = jnp.einsum("hqk,khd->hqd", probs_low, value_window)
        delta = jnp.sum(jnp.transpose(grad_block, (1, 0, 2)) * attended, axis=2, keepdims=True)
        dprobs = jnp.einsum("qhd,khd->hqk", grad_block, value_window)
        dscores = low_round(probs * (dprobs - delta))
        query_grad = (jnp.einsum("hqk,khd->qhd", dscores, key_window) * softmax_scale).reshape(shard_rows, width).astype(jnp.bfloat16)
        key_part = low_round(jnp.einsum("hqk,qhd->khd", dscores, query_block) * softmax_scale).reshape(window_rows, width)
        value_part = low_round(jnp.einsum("hqk,qhd->khd", probs_low, grad_block)).reshape(window_rows, width)
        update = jnp.stack([key_part, value_part])
        current = lax.dynamic_slice_in_dim(carry, first_row, window_rows, 1)
        carry = lax.dynamic_update_slice_in_dim(carry, current + update, first_row, 1)
        return carry, query_grad

    start_sums = jnp.zeros((2, TOKENS + 2 * pad_rows, width), jnp.float32)
    sums, query_grads = lax.scan(one_shard, start_sums, jnp.arange(N_SEQ, dtype=jnp.int32))
    query_grad_all = query_grads.reshape(TOKENS, width)
    group_width = width // N_HEAD
    total = jnp.zeros((TOKENS, D), jnp.float32)
    for group in range(N_HEAD):
        columns = slice(group * group_width, (group + 1) * group_width)
        part = jnp.dot(query_grad_all[:, columns], query_weight[:, columns].T, preferred_element_type=jnp.float32)
        total = total + low_round(part)
    input_grad = total.astype(jnp.bfloat16)
    key_grad = sums[0, pad_rows:pad_rows + TOKENS].astype(jnp.bfloat16)
    value_grad = sums[1, pad_rows:pad_rows + TOKENS].astype(jnp.bfloat16)
    return (input_grad, key_grad, value_grad)
```

```python
import functools

import jax
import jax.numpy as jnp
from jax import lax
from jax.experimental import pallas as pl
from jax.experimental.pallas import tpu as pltpu
from jax.sharding import PartitionSpec as P

HEAD_DIM = 128
HEADS_DEV = 3
TILE = 128
TILES_DEV = 2
SCALE = HEAD_DIM ** (-0.5)
BLOCKS = 6


def move(block, route):
    size = lax.axis_size("seq")
    pairs = [(i, route(i)) for i in range(size)]
    return lax.ppermute(block, "seq", [(i, j) for i, j in pairs if 0 <= j < size])


def to_core(i):
    return i ^ 1


def to_frame_pair(i):
    return i ^ 2


def to_next_pair(i):
    return i + 4 if i % 4 < 2 else i - 4


def live_tiles(lists, counts, targets):
    slots = jnp.arange(lists.shape[1], dtype=jnp.int32)
    used = slots[None, :] < counts[:, None]
    hits = (lists[:, :, None] == targets[None, None, :]) & used[:, :, None]
    return jnp.any(hits, axis=1)


def masks(position, lists, counts):
    tiles = lists.shape[0]
    frame_even = position % 4 < 2
    far = jnp.where(frame_even, position - 2, position + 2)
    owners = jnp.stack([position, position ^ 1, position ^ 2, position ^ 3, far, far ^ 1])
    pair = jnp.arange(TILES_DEV, dtype=jnp.int32)
    window = (owners[:, None] * TILES_DEV + pair[None, :]).reshape(-1)
    own = position * TILES_DEV + pair
    live = live_tiles(lists, counts, jnp.arange(tiles, dtype=jnp.int32))
    every = jnp.arange(tiles, dtype=jnp.int32)
    pick_window = window[:, None] == every[None, :]
    pick_own = own[:, None] == every[None, :]
    as_query = jnp.any(pick_own[:, :, None] & live[None, :, :], axis=1)
    own_to_window = jnp.any(as_query[:, None, :] & pick_window[None, :, :], axis=2)
    from_window = jnp.any(pick_window[:, :, None] & live[None, :, :], axis=1)
    window_to_own = jnp.any(from_window[:, None, :] & pick_own[None, :, :], axis=2)
    lanes = functools.partial(jnp.repeat, repeats=TILE, axis=-1)
    first = jnp.where(own_to_window.T, 0.0, -jnp.inf).astype(jnp.float32)
    first = lanes(first).reshape(BLOCKS, TILES_DEV, TILES_DEV * TILE)
    second = jnp.where(window_to_own, 0.0, -jnp.inf).astype(jnp.float32)
    second = second.reshape(BLOCKS, TILES_DEV, TILES_DEV).transpose(0, 2, 1)
    return first, lanes(second)


def nt(left, right):
    return lax.dot_general(
        left, right, (((1,), (1,)), ((), ())), preferred_element_type=jnp.float32
    )


def tn(left, right):
    return lax.dot_general(
        left, right, (((0,), (0,)), ((), ())), preferred_element_type=jnp.float32
    )


def add_mask(scores, mask):
    rows, lanes = scores.shape
    split = scores.reshape(TILES_DEV, rows // TILES_DEV, lanes)
    return (split + mask[:, None, :]).reshape(rows, lanes)


def query_kernel(
    mask_ref, q_ref, g_ref, k_ref, v_ref, b1, b2, b3, b4, b5, dq_ref, stat_ref, s_ref, d_ref
):
    query = q_ref[...]
    grad = g_ref[...]
    pairs = [b1, b2, b3, b4, b5]

    def key(b):
        return k_ref[...] if b == 0 else pairs[b - 1][0]

    def value(b):
        return v_ref[...] if b == 0 else pairs[b - 1][1]

    top = None
    for b in range(BLOCKS):
        scores = add_mask(nt(key(b), query) * SCALE, mask_ref[b])
        s_ref[b] = scores
        d_ref[b] = nt(value(b), grad)
        peak = jnp.max(scores, axis=0, keepdims=True)
        top = peak if top is None else jnp.maximum(top, peak)
    total = jnp.zeros_like(top)
    for b in range(BLOCKS):
        weight = jnp.exp(s_ref[b] - top)
        s_ref[b] = weight
        total = total + jnp.sum(weight, axis=0, keepdims=True)
    inverse = 1.0 / total
    delta = jnp.zeros_like(top)
    for b in range(BLOCKS):
        probs = s_ref[b] * inverse
        s_ref[b] = probs
        low = probs.astype(jnp.bfloat16).astype(jnp.float32)
        delta = delta + jnp.sum(low * d_ref[b], axis=0, keepdims=True)
    acc = jnp.zeros(query.shape, jnp.float32)
    for b in range(BLOCKS):
        dscores = (s_ref[b] * (d_ref[b] - delta)).astype(jnp.bfloat16)
        acc = acc + tn(dscores, key(b))
    dq_ref[...] = (acc * SCALE).astype(jnp.bfloat16)
    row = lax.broadcasted_iota(jnp.int32, stat_ref.shape[1:], 0)
    stat_ref[0] = jnp.where(row == 0, top + jnp.log(total), delta)


def key_kernel(
    mask_ref, k_ref, v_ref, q_ref, g_ref, b1, b2, b3, b4, b5,
    t0, t1, t2, t3, t4, t5, dk_ref, dv_ref,
):
    key = k_ref[...]
    value = v_ref[...]
    pairs = [b1, b2, b3, b4, b5]
    stats = [t0, t1, t2, t3, t4, t5]
    key_acc = jnp.zeros(key.shape, jnp.float32)
    value_acc = jnp.zeros(key.shape, jnp.float32)
    for b in range(BLOCKS):
        query = q_ref[...] if b == 0 else pairs[b - 1][0]
        grad = g_ref[...] if b == 0 else pairs[b - 1][1]
        stat = stats[b][0]
        scores = add_mask(nt(key, query) * SCALE, mask_ref[b])
        probs = jnp.exp(scores - stat[0:1])
        dscores = (probs * (nt(value, grad) - stat[1:2])).astype(jnp.bfloat16)
        low = probs.astype(jnp.bfloat16)
        value_acc = value_acc + jnp.dot(low, grad, preferred_element_type=jnp.float32)
        key_acc = key_acc + jnp.dot(dscores, query, preferred_element_type=jnp.float32)
    dk_ref[...] = (key_acc * SCALE).astype(jnp.bfloat16)
    dv_ref[...] = value_acc.astype(jnp.bfloat16)


def head_columns(rows):
    return pl.BlockSpec((rows, HEAD_DIM), lambda h: (0, h))


def head_pair(rows):
    return pl.BlockSpec((2, rows, HEAD_DIM), lambda h: (0, 0, h))


def query_pass(mask, queries, out_grad, keys, values, pairs):
    rows, width = queries.shape
    col = head_columns(rows)
    return pl.pallas_call(
        query_kernel,
        grid=(HEADS_DEV,),
        in_specs=[pl.BlockSpec(mask.shape, lambda h: (0, 0, 0)), col, col, col, col]
        + [head_pair(rows)] * 5,
        out_specs=[col, pl.BlockSpec((1, 8, rows), lambda h: (h, 0, 0))],
        out_shape=[
            jax.ShapeDtypeStruct((rows, width), jnp.bfloat16),
            jax.ShapeDtypeStruct((HEADS_DEV, 8, rows), jnp.float32),
        ],
        scratch_shapes=[pltpu.VMEM((BLOCKS, rows, rows), jnp.float32)] * 2,
        name="query_pass",
    )(mask, queries, out_grad, keys, values, *pairs)


def key_pass(mask, keys, values, queries, out_grad, pairs, stats):
    rows, width = queries.shape
    col = head_columns(rows)
    stat = pl.BlockSpec((1, 8, rows), lambda h: (h, 0, 0))
    return pl.pallas_call(
        key_kernel,
        grid=(HEADS_DEV,),
        in_specs=[pl.BlockSpec(mask.shape, lambda h: (0, 0, 0)), col, col, col, col]
        + [head_pair(rows)] * 5 + [stat] * 6,
        out_specs=[col, col],
        out_shape=[jax.ShapeDtypeStruct((rows, width), jnp.bfloat16)] * 2,
        name="key_pass",
    )(mask, keys, values, queries, out_grad, *pairs, *stats)


def input_kernel(place_ref, q_ref, x_ref, *refs):
    pieces = refs[:8]
    out_ref, w_ref, sems = refs[8:]
    rows = pieces[0].shape[1]
    copies = []
    for i, piece in enumerate(pieces):
        for j in range(2):
            at = pl.multiple_of(place_ref[i % 4, j] * rows, 64)
            copy = pltpu.make_async_copy(
                piece.at[j], w_ref.at[i // 4, pl.ds(at, rows)], sems.at[2 * i + j]
            )
            copy.start()
            copies.append(copy)
    for copy in copies:
        copy.wait()
    chunk = 512
    own = q_ref[...]
    other = x_ref[...]
    for at in range(0, out_ref.shape[1], chunk):
        part = nt(own, w_ref[0, at : at + chunk]) + nt(other, w_ref[1, at : at + chunk])
        out_ref[:, at : at + chunk] = part.astype(jnp.bfloat16)


def input_pass(place, own, other, pieces):
    rows, width = own.shape
    out_width = pieces[0].shape[1] * 8
    vmem = pl.BlockSpec(memory_space=pltpu.VMEM)
    return pl.pallas_call(
        input_kernel,
        in_specs=[pl.BlockSpec(memory_space=pltpu.SMEM), vmem, vmem]
        + [pl.BlockSpec(memory_space=pl.ANY)] * 8,
        out_specs=vmem,
        out_shape=jax.ShapeDtypeStruct((rows, out_width), jnp.bfloat16),
        scratch_shapes=[
            pltpu.VMEM((2, out_width, width), jnp.bfloat16),
            pltpu.SemaphoreType.DMA((16,)),
        ],
        name="input_pass",
    )(place, own, other, *pieces)


def spread_weight(weight, position, group):
    by_one = move(weight, lambda i: i ^ 4)
    by_two = move(weight, lambda i: i ^ 8)
    by_three = move(weight, lambda i: i ^ 12)
    near = jnp.stack([weight, by_one])
    away = jnp.stack([by_two, by_three])
    same = position // 8 == group
    kept = jnp.where(same, near, away)
    sent = jnp.where(same, away, near)
    swapped = lax.ppermute(sent, "head", [(0, 1), (1, 0)])
    pieces = []
    for held in (kept, swapped):
        paired = move(held, to_frame_pair)
        pieces += [held, move(held, to_core), paired, move(paired, to_core)]
    base = position % 8
    hop = jnp.arange(4, dtype=jnp.int32)
    block = base ^ hop
    return pieces, jnp.stack([block, block ^ 4], axis=1)


def input_by_gather(query_grad, weight):
    size, groups = lax.axis_size("seq"), lax.axis_size("head")
    part = size // groups
    route = []
    for p in range(size):
        for c in range(groups):
            high, low = divmod(p, part)
            route.append((p * groups + c, (c * part + low) * groups + high))
    regrouped = lax.ppermute(weight, ("seq", "head"), route)
    gathered = lax.all_gather(regrouped, "seq", axis=0, tiled=True)
    gathered = gathered.reshape(groups, -1, weight.shape[1])
    rows = lax.all_gather(query_grad, "head")
    total = jnp.einsum("grk,gck->rc", rows, gathered, preferred_element_type=jnp.float32)
    return total.astype(jnp.bfloat16)


def per_device(
    queries, key_rows, value_rows, out_grad, query_weight, neighbour_tiles, neighbour_count
):
    position = lax.axis_index("seq")
    direct = lax.axis_size("seq") == 16 and lax.axis_size("head") == 2
    if direct:
        pieces, place = spread_weight(query_weight, position, lax.axis_index("head"))
    query_mask, key_mask = masks(position, neighbour_tiles, neighbour_count)

    def window(pair):
        near = move(pair, to_frame_pair)
        far = move(near, to_next_pair)
        return [move(pair, to_core), near, move(near, to_core), far, move(far, to_core)]

    kv_pairs = window(jnp.stack([key_rows, value_rows]))
    qg_pairs = window(jnp.stack([queries, out_grad]))
    query_grad, stats = query_pass(
        query_mask, queries, out_grad, key_rows, value_rows, kv_pairs
    )
    if direct:
        swapped = lax.ppermute(query_grad, "head", [(0, 1), (1, 0)])
        input_grad = input_pass(place, query_grad, swapped, pieces)
    else:
        input_grad = input_by_gather(query_grad, query_weight)
    key_grad, value_grad = key_pass(
        key_mask, key_rows, value_rows, queries, out_grad, qg_pairs, [stats] + window(stats)
    )
    return (input_grad, key_grad, value_grad)


def solution(mesh):
    placed = (
        P("seq", "head"),
        P("seq", "head"),
        P("seq", "head"),
        P("seq", "head"),
        P("seq", "head"),
        P(),
        P(),
    )
    return jax.shard_map(
        per_device,
        mesh=mesh,
        in_specs=placed,
        out_specs=(P("seq", "head"), P("seq", "head"), P("seq", "head")),
        check_vma=False,
    )
```

```python
import jax
import jax.numpy as jnp
from jax import lax
from jax.experimental import pallas as pl
from jax.experimental.pallas import tpu as pltpu
from jax.sharding import PartitionSpec as P

HEAD_DIM = 128
HEADS_DEV = 3
TILE = 128
TILES_DEV = 2
SCALE = HEAD_DIM ** (-0.5)
LOG2_E = 1.4426950408889634
SCALE_2 = SCALE * LOG2_E
BLOCKS = 6
DEAD = -64


def move(block, route):
    size = lax.axis_size("seq")
    pairs = [(i, route(i)) for i in range(size)]
    return lax.ppermute(block, "seq", [(i, j) for i, j in pairs if 0 <= j < size])


def swap_groups(block):
    return lax.ppermute(block, "head", [(0, 1), (1, 0)])


def to_core(i):
    return i ^ 1


def to_frame_pair(i):
    return i ^ 2


def to_next_pair(i):
    return i + 4 if i % 4 < 2 else i - 4


def owners(position):
    far = jnp.where(position % 4 < 2, position - 2, position + 2)
    return [position, position ^ 1, position ^ 2, position ^ 3, far, far ^ 1]


def nt(left, right):
    return lax.dot_general(
        left, right, (((1,), (1,)), ((), ())), preferred_element_type=jnp.float32
    )


def tn(left, right):
    return lax.dot_general(
        left, right, (((0,), (0,)), ((), ())), preferred_element_type=jnp.float32
    )


def any_lane(hits):
    best = jnp.max(jnp.where(hits, 1.0, 0.0), axis=1, keepdims=True)
    return jnp.where(best > 0.0, 0.0, -jnp.inf)


def own_query_masks(position, lists_ref, mask_ref):
    row = lax.broadcasted_iota(jnp.int32, (16, lists_ref.shape[1]), 0)
    tile = jnp.full(row.shape, 2 * DEAD, jnp.int32)
    for b, owner in enumerate(owners(position)):
        tile = jnp.where(row // TILES_DEV == b, owner * TILES_DEV + row % TILES_DEV, tile)
    for c in range(TILES_DEV):
        own = lists_ref[pl.ds(position * TILES_DEV + c, 1)]
        mask_ref[c] = jnp.broadcast_to(any_lane(own == tile), mask_ref.shape[1:])


def own_key_masks(position, lists_ref, mask_ref):
    for a in range(TILES_DEV):
        hits = lists_ref[...] == position * TILES_DEV + a
        mask_ref[a] = jnp.broadcast_to(any_lane(hits), mask_ref.shape[1:])


def query_kernel(
    at_ref, lists_ref, q_ref, g_ref, k_ref, v_ref, b1, b2, b3, b4, b5,
    dq_ref, stat_ref, s_ref, d_ref, mask_ref,
):
    own_query_masks(at_ref[0], lists_ref, mask_ref)
    stat_ref[...] = jnp.zeros_like(stat_ref)
    half = q_ref.shape[0] // TILES_DEV
    pairs = [b1, b2, b3, b4, b5]
    tiles = [(b, a) for b in range(BLOCKS) for a in range(TILES_DEV)]

    def mask(b, a):
        at = TILES_DEV * b + a
        return jnp.concatenate([mask_ref[0, at : at + 1], mask_ref[1, at : at + 1]], axis=1)

    for head in range(HEADS_DEV):
        cols = slice(head * HEAD_DIM, (head + 1) * HEAD_DIM)
        query = q_ref[:, cols]
        grad = g_ref[:, cols]

        def key(b):
            return k_ref[:, cols] if b == 0 else pairs[b - 1][0, :, cols]

        def value(b):
            return v_ref[:, cols] if b == 0 else pairs[b - 1][1, :, cols]

        top = None
        for b in range(BLOCKS):
            scores = nt(key(b), query)
            s_ref[b] = scores
            d_ref[b] = nt(value(b), grad)
            for a in range(TILES_DEV):
                peak = jnp.max(scores[a * half : (a + 1) * half], axis=0, keepdims=True)
                peak = peak * SCALE_2 + mask(b, a)
                top = peak if top is None else jnp.maximum(top, peak)
        total = jnp.zeros_like(top)
        delta = jnp.zeros_like(top)
        for b, a in tiles:
            part = slice(a * half, (a + 1) * half)
            weight = jnp.exp2(s_ref[b, part] * SCALE_2 - (top - mask(b, a)))
            s_ref[b, part] = weight
            total = total + jnp.sum(weight, axis=0, keepdims=True)
            delta = delta + jnp.sum(weight * d_ref[b, part], axis=0, keepdims=True)
        inverse = 1.0 / total
        delta = delta * inverse
        acc = jnp.zeros((HEAD_DIM, query.shape[0]), jnp.float32)
        for b in range(BLOCKS):
            dscores = (s_ref[b] * (d_ref[b] - delta)).astype(jnp.bfloat16)
            acc = acc + tn(key(b), dscores)
        dq_ref[:, cols] = (acc * (inverse * SCALE)).T.astype(jnp.bfloat16)
        stat_ref[head : head + 1] = top + jnp.log(total) * LOG2_E
        stat_ref[head + HEADS_DEV : head + HEADS_DEV + 1] = delta


def key_kernel(
    at_ref, lists_ref, k_ref, v_ref, q_ref, g_ref, b1, b2, b3, b4, b5,
    t0, t1, t2, t4, dk_ref, dv_ref, mask_ref,
):
    tiles = lists_ref.shape[0]
    own_key_masks(at_ref[0], lists_ref, mask_ref)
    half = k_ref.shape[0] // TILES_DEV
    pairs = [b1, b2, b3, b4, b5]
    stats = [(t0, 0), (t1, 0), (t2, 0), (t2, 8), (t4, 0), (t4, 8)]
    masks = []
    for owner in owners(at_ref[0]):
        first = owner * TILES_DEV
        inside = (first >= 0) & (first < tiles)
        there = jnp.where(inside, 0.0, -jnp.inf)
        row = jnp.where(inside, first, 0)
        masks.append([
            jnp.concatenate([mask_ref[a, pl.ds(row + c, 1)] for c in range(TILES_DEV)], axis=1)
            + there
            for a in range(TILES_DEV)
        ])
    for head in range(HEADS_DEV):
        cols = slice(head * HEAD_DIM, (head + 1) * HEAD_DIM)
        key = k_ref[:, cols]
        value = v_ref[:, cols]
        key_acc = jnp.zeros(key.shape, jnp.float32)
        value_acc = jnp.zeros(key.shape, jnp.float32)
        for b in range(BLOCKS):
            query = q_ref[:, cols] if b == 0 else pairs[b - 1][0, :, cols]
            grad = g_ref[:, cols] if b == 0 else pairs[b - 1][1, :, cols]
            stat, at = stats[b]
            log_norm = stat[at + head : at + head + 1]
            at += HEADS_DEV
            delta = stat[at + head : at + head + 1]
            scores = nt(key, query)
            dprobs = nt(value, grad)
            low, dscores = [], []
            for a in range(TILES_DEV):
                part = slice(a * half, (a + 1) * half)
                probs = jnp.exp2(scores[part] * SCALE_2 - (log_norm - masks[b][a]))
                low.append(probs.astype(jnp.bfloat16))
                dscores.append((probs * (dprobs[part] - delta)).astype(jnp.bfloat16))
            low = jnp.concatenate(low, axis=0)
            dscores = jnp.concatenate(dscores, axis=0)
            value_acc = value_acc + jnp.dot(low, grad, preferred_element_type=jnp.float32)
            key_acc = key_acc + jnp.dot(dscores, query, preferred_element_type=jnp.float32)
        dk_ref[:, cols] = (key_acc * SCALE).astype(jnp.bfloat16)
        dv_ref[:, cols] = value_acc.astype(jnp.bfloat16)


SMEM = pl.BlockSpec(memory_space=pltpu.SMEM)
VMEM = pl.BlockSpec(memory_space=pltpu.VMEM)
ANYWHERE = pl.BlockSpec(memory_space=pl.ANY)


def query_pass(at, lists, queries, out_grad, keys, values, pairs):
    rows, width = queries.shape
    return pl.pallas_call(
        query_kernel,
        in_specs=[SMEM] + [VMEM] * 10,
        out_specs=[VMEM] * 2,
        out_shape=[
            jax.ShapeDtypeStruct((rows, width), jnp.bfloat16),
            jax.ShapeDtypeStruct((8, rows), jnp.float32),
        ],
        scratch_shapes=[pltpu.VMEM((BLOCKS, rows, rows), jnp.float32)] * 2
        + [pltpu.VMEM((TILES_DEV, 16, TILE), jnp.float32)],
        name="query_pass",
    )(at, lists, queries, out_grad, keys, values, *pairs)


def key_pass(at, lists, keys, values, queries, out_grad, pairs, stats):
    rows, width = queries.shape
    return pl.pallas_call(
        key_kernel,
        in_specs=[SMEM] + [VMEM] * 14,
        out_specs=[VMEM] * 2,
        out_shape=[jax.ShapeDtypeStruct((rows, width), jnp.bfloat16)] * 2,
        scratch_shapes=[pltpu.VMEM((TILES_DEV, lists.shape[0], TILE), jnp.float32)],
        name="key_pass",
    )(at, lists, keys, values, queries, out_grad, *pairs, *stats)


def pack_kernel(slots_ref, counts_ref, k_ref, v_ref, q_ref, g_ref, kv_ref, qg_ref, lists_ref):
    kv_ref[0] = k_ref[...]
    kv_ref[1] = v_ref[...]
    qg_ref[0] = q_ref[...]
    qg_ref[1] = g_ref[...]
    slots, tiles = slots_ref.shape
    side = 128
    for first in range(0, tiles, side):
        width = min(side, tiles - first)
        block = slots_ref[:, first : first + width]
        used = lax.broadcasted_iota(jnp.int32, block.shape, 0) < counts_ref[:, first : first + width]
        block = jnp.where(used, block, DEAD)
        block = jnp.concatenate([block, jnp.full((16 - slots, width), DEAD, jnp.int32)], axis=0)
        if width < side:
            block = jnp.concatenate([block, jnp.full((16, side - width), DEAD, jnp.int32)], axis=1)
        block = jnp.concatenate([block, jnp.full((side - 16, side), DEAD, jnp.int32)], axis=0)
        lists_ref[first : first + width] = block.T[:width]


def pack(slots, counts, keys, values, queries, out_grad):
    pair = jax.ShapeDtypeStruct((2,) + keys.shape, keys.dtype)
    return pl.pallas_call(
        pack_kernel,
        in_specs=[VMEM] * 6,
        out_specs=[VMEM] * 3,
        out_shape=[pair, pair, jax.ShapeDtypeStruct((slots.shape[1], 128), jnp.int32)],
        name="pack",
    )(slots, counts, keys, values, queries, out_grad)


def start_input(at_ref, pieces, w_ref, sems):
    rows = pieces[0].shape[1]
    copies = []
    for j in range(2):
        for i, piece in enumerate(pieces):
            place = (at_ref[0] % 4) ^ (i % 4)
            copy = pltpu.make_async_copy(
                piece.at[j],
                w_ref.at[j, i // 4, pl.ds(pl.multiple_of(place * rows, 64), rows)],
                sems.at[8 * j + i],
            )
            copy.start()
            copies.append(copy)
    return copies


def finish_input(at_ref, q_ref, x_ref, copies, w_ref, o_ref, out_ref, sems):
    span = w_ref.shape[2]
    own = q_ref[...]
    other = x_ref[...]
    outs = []
    for j in range(2):
        for copy in copies[8 * j : 8 * j + 8]:
            copy.wait()
        part = nt(own, w_ref[j, 0]) + nt(other, w_ref[j, 1])
        o_ref[j] = part.astype(o_ref.dtype)
        first = pl.multiple_of((at_ref[0] % 8 // 4 ^ j) * span, span)
        copy = pltpu.make_async_copy(o_ref.at[j], out_ref.at[:, pl.ds(first, span)], sems.at[j])
        copy.start()
        outs.append(copy)
    for copy in outs:
        copy.wait()


def input_kernel(at_ref, own_ref, other_ref, *refs):
    pieces = refs[:8]
    out_ref, w_ref, o_ref, sems, out_sems = refs[8:]
    copies = start_input(at_ref, pieces, w_ref, sems)
    finish_input(at_ref, own_ref, other_ref, copies, w_ref, o_ref, out_ref, out_sems)


def input_pass(at, own, other, pieces):
    rows, width = own.shape
    span = pieces[0].shape[1] * 4
    return pl.pallas_call(
        input_kernel,
        in_specs=[SMEM, VMEM, VMEM] + [ANYWHERE] * 8,
        out_specs=ANYWHERE,
        out_shape=jax.ShapeDtypeStruct((rows, 2 * span), jnp.bfloat16),
        scratch_shapes=[
            pltpu.VMEM((2, 2, span, width), jnp.bfloat16),
            pltpu.VMEM((2, rows, span), jnp.bfloat16),
            pltpu.SemaphoreType.DMA((16,)),
            pltpu.SemaphoreType.DMA((2,)),
        ],
        name="input_pass",
    )(at, own, other, *pieces)


def spread_weight(weight, position, group):
    by_one = move(weight, lambda i: i ^ 4)
    by_two = move(weight, lambda i: i ^ 8)
    middle = move(weight, lambda i: i ^ 12 if 4 <= i < 12 else -1)
    outer = move(by_two, lambda i: i ^ 4 if 4 <= i < 12 else -1)
    by_three = jnp.where((position >= 4) & (position < 12), middle, outer)
    near = jnp.stack([weight, by_one])
    away = jnp.stack([by_two, by_three])
    same = position // 8 == group
    kept = jnp.where(same, near, away)
    sent = jnp.where(same, away, near)
    swapped = swap_groups(sent)
    pieces = []
    for held in (kept, swapped):
        paired = move(held, to_frame_pair)
        core = move(held, to_core)
        pieces += [held, core, paired, move(paired, to_core)]
    return pieces


def input_by_gather(query_grad, weight):
    size, groups = lax.axis_size("seq"), lax.axis_size("head")
    part = size // groups
    route = []
    for p in range(size):
        for c in range(groups):
            high, low = divmod(p, part)
            route.append((p * groups + c, (c * part + low) * groups + high))
    regrouped = lax.ppermute(weight, ("seq", "head"), route)
    gathered = lax.all_gather(regrouped, "seq", axis=0, tiled=True)
    gathered = gathered.reshape(groups, -1, weight.shape[1])
    rows = lax.all_gather(query_grad, "head")
    total = jnp.einsum("grk,gck->rc", rows, gathered, preferred_element_type=jnp.float32)
    return total.astype(jnp.bfloat16)


def gradients(
    queries, key_rows, value_rows, out_grad, query_weight, neighbour_tiles, neighbour_count
):
    position = lax.axis_index("seq")
    direct = lax.axis_size("seq") == 16 and lax.axis_size("head") == 2
    kv_pair, qg_pair, lists = pack(
        neighbour_tiles.T, neighbour_count[None], key_rows, value_rows, queries, out_grad
    )
    if direct:
        pieces = spread_weight(query_weight, position, lax.axis_index("head"))
    at = jnp.full((1,), position, jnp.int32)

    def window(pair):
        near = move(pair, to_frame_pair)
        far = move(near, to_next_pair)
        core = move(pair, to_core)
        near_core = move(near, to_core)
        return [core, near, near_core, far, move(far, to_core)]

    kv_pairs = window(kv_pair)
    qg_pairs = window(qg_pair)
    query_grad, own = query_pass(
        at, lists, queries, out_grad, key_rows, value_rows, kv_pairs
    )
    core = move(own, to_core)
    near = move(jnp.concatenate([own, core]), to_frame_pair)
    stats = [own, core, near, move(near, to_next_pair)]
    if direct:
        swapped = swap_groups(query_grad)
        input_grad = input_pass(at, query_grad, swapped, pieces)
    else:
        input_grad = input_by_gather(query_grad, query_weight)
    key_grad, value_grad = key_pass(
        at, lists, key_rows, value_rows, queries, out_grad, qg_pairs, stats
    )
    return (input_grad, key_grad, value_grad)


def solution(mesh):
    placed = (
        P("seq", "head"),
        P("seq", "head"),
        P("seq", "head"),
        P("seq", "head"),
        P("seq", "head"),
        P(),
        P(),
    )
    return jax.shard_map(
        gradients,
        mesh=mesh,
        in_specs=placed,
        out_specs=(P("seq", "head"), P("seq", "head"), P("seq", "head")),
        check_vma=False,
    )
```

```python
import jax
import jax.numpy as jnp
from jax import lax
from jax.experimental import pallas as pl
from jax.experimental.pallas import tpu as pltpu
from jax.sharding import PartitionSpec as P

HEAD_DIM = 128
HEADS_DEV = 3
TILE = 128
TILES_DEV = 2
SCALE = HEAD_DIM ** (-0.5)
LOG2_E = 1.4426950408889634
SCALE_2 = SCALE * LOG2_E
BLOCKS = 6
DEAD = -64


def move(block, route):
    size = lax.axis_size("seq")
    pairs = [(i, route(i)) for i in range(size)]
    return lax.ppermute(block, "seq", [(i, j) for i, j in pairs if 0 <= j < size])


def swap_groups(block):
    return lax.ppermute(block, "head", [(0, 1), (1, 0)])


def to_core(i):
    return i ^ 1


def to_frame_pair(i):
    return i ^ 2


def to_next_pair(i):
    return i + 4 if i % 4 < 2 else i - 4


def to_far_pair(i):
    return i - 2 if i % 4 < 2 else i + 2


def owners(position):
    far = jnp.where(position % 4 < 2, position - 2, position + 2)
    return [position, position ^ 1, position ^ 2, position ^ 3, far, far ^ 1]


def nt(left, right):
    return lax.dot_general(
        left, right, (((1,), (1,)), ((), ())), preferred_element_type=jnp.float32
    )


def tn(left, right):
    return lax.dot_general(
        left, right, (((0,), (0,)), ((), ())), preferred_element_type=jnp.float32
    )


def any_lane(hits):
    best = jnp.max(jnp.where(hits, 1.0, 0.0), axis=1, keepdims=True)
    return jnp.where(best > 0.0, 0.0, -jnp.inf)


def own_query_masks(position, lists_ref, mask_ref):
    row = lax.broadcasted_iota(jnp.int32, (16, lists_ref.shape[1]), 0)
    tile = jnp.full(row.shape, 2 * DEAD, jnp.int32)
    for b, owner in enumerate(owners(position)):
        tile = jnp.where(row // TILES_DEV == b, owner * TILES_DEV + row % TILES_DEV, tile)
    for c in range(TILES_DEV):
        own = lists_ref[pl.ds(position * TILES_DEV + c, 1)]
        mask_ref[c] = jnp.broadcast_to(any_lane(own == tile), mask_ref.shape[1:])


def own_key_masks(position, lists_ref, mask_ref):
    for a in range(TILES_DEV):
        hits = lists_ref[...] == position * TILES_DEV + a
        mask_ref[a] = jnp.broadcast_to(any_lane(hits), mask_ref.shape[1:])


def query_kernel(
    at_ref, lists_ref, q_ref, g_ref, k_ref, v_ref, b1, b2, b3, b4, b5,
    dq_ref, stat_ref, s_ref, d_ref, mask_ref,
):
    own_query_masks(at_ref[0], lists_ref, mask_ref)
    stat_ref[...] = jnp.zeros_like(stat_ref)
    half = q_ref.shape[0] // TILES_DEV
    pairs = [b1, b2, b3, b4, b5]
    tiles = [(b, a) for b in range(BLOCKS) for a in range(TILES_DEV)]

    def mask(b, a):
        at = TILES_DEV * b + a
        return jnp.concatenate([mask_ref[0, at : at + 1], mask_ref[1, at : at + 1]], axis=1)

    for head in range(HEADS_DEV):
        cols = slice(head * HEAD_DIM, (head + 1) * HEAD_DIM)
        query = q_ref[:, cols]
        grad = g_ref[:, cols]

        def key(b):
            return k_ref[:, cols] if b == 0 else pairs[b - 1][0, :, cols]

        def value(b):
            return v_ref[:, cols] if b == 0 else pairs[b - 1][1, :, cols]

        top = None
        for b in range(BLOCKS):
            scores = nt(key(b), query)
            s_ref[b] = scores
            d_ref[b] = nt(value(b), grad)
            for a in range(TILES_DEV):
                peak = jnp.max(scores[a * half : (a + 1) * half], axis=0, keepdims=True)
                peak = peak * SCALE_2 + mask(b, a)
                top = peak if top is None else jnp.maximum(top, peak)
        total = jnp.zeros_like(top)
        delta = jnp.zeros_like(top)
        for b, a in tiles:
            part = slice(a * half, (a + 1) * half)
            weight = jnp.exp2(s_ref[b, part] * SCALE_2 - (top - mask(b, a)))
            s_ref[b, part] = weight
            total = total + jnp.sum(weight, axis=0, keepdims=True)
            delta = delta + jnp.sum(weight * d_ref[b, part], axis=0, keepdims=True)
        inverse = 1.0 / total
        delta = delta * inverse
        acc = jnp.zeros((HEAD_DIM, query.shape[0]), jnp.float32)
        for b in range(BLOCKS):
            dscores = (s_ref[b] * (d_ref[b] - delta)).astype(jnp.bfloat16)
            acc = acc + tn(key(b), dscores)
        dq_ref[:, cols] = (acc * (inverse * SCALE)).T.astype(jnp.bfloat16)
        stat_ref[head : head + 1] = top + jnp.log(total) * LOG2_E
        stat_ref[head + HEADS_DEV : head + HEADS_DEV + 1] = delta


def key_kernel(
    at_ref, lists_ref, k_ref, v_ref, q_ref, g_ref, b1, b2, b3, b4, b5,
    t0, t1, t2, t4, dk_ref, dv_ref, mask_ref,
):
    tiles = lists_ref.shape[0]
    own_key_masks(at_ref[0], lists_ref, mask_ref)
    half = k_ref.shape[0] // TILES_DEV
    pairs = [b1, b2, b3, b4, b5]
    stats = [(t0, 0), (t1, 0), (t2, 0), (t2, 8), (t4, 0), (t4, 8)]
    masks = []
    for owner in owners(at_ref[0]):
        first = owner * TILES_DEV
        inside = (first >= 0) & (first < tiles)
        there = jnp.where(inside, 0.0, -jnp.inf)
        row = jnp.where(inside, first, 0)
        masks.append([
            jnp.concatenate([mask_ref[a, pl.ds(row + c, 1)] for c in range(TILES_DEV)], axis=1)
            + there
            for a in range(TILES_DEV)
        ])
    for head in range(HEADS_DEV):
        cols = slice(head * HEAD_DIM, (head + 1) * HEAD_DIM)
        key = k_ref[:, cols]
        value = v_ref[:, cols]
        key_acc = jnp.zeros(key.shape, jnp.float32)
        value_acc = jnp.zeros(key.shape, jnp.float32)
        for b in range(BLOCKS):
            query = q_ref[:, cols] if b == 0 else pairs[b - 1][0, :, cols]
            grad = g_ref[:, cols] if b == 0 else pairs[b - 1][1, :, cols]
            stat, at = stats[b]
            log_norm = stat[at + head : at + head + 1]
            at += HEADS_DEV
            delta = stat[at + head : at + head + 1]
            scores = nt(key, query)
            dprobs = nt(value, grad)
            low, dscores = [], []
            for a in range(TILES_DEV):
                part = slice(a * half, (a + 1) * half)
                probs = jnp.exp2(scores[part] * SCALE_2 - (log_norm - masks[b][a]))
                low.append(probs.astype(jnp.bfloat16))
                dscores.append((probs * (dprobs[part] - delta)).astype(jnp.bfloat16))
            low = jnp.concatenate(low, axis=0)
            dscores = jnp.concatenate(dscores, axis=0)
            value_acc = value_acc + jnp.dot(low, grad, preferred_element_type=jnp.float32)
            key_acc = key_acc + jnp.dot(dscores, query, preferred_element_type=jnp.float32)
        dk_ref[:, cols] = (key_acc * SCALE).astype(jnp.bfloat16)
        dv_ref[:, cols] = value_acc.astype(jnp.bfloat16)


SMEM = pl.BlockSpec(memory_space=pltpu.SMEM)
VMEM = pl.BlockSpec(memory_space=pltpu.VMEM)
ANYWHERE = pl.BlockSpec(memory_space=pl.ANY)


def query_pass(at, lists, queries, out_grad, keys, values, pairs):
    rows, width = queries.shape
    return pl.pallas_call(
        query_kernel,
        in_specs=[SMEM] + [VMEM] * 10,
        out_specs=[VMEM] * 2,
        out_shape=[
            jax.ShapeDtypeStruct((rows, width), jnp.bfloat16),
            jax.ShapeDtypeStruct((8, rows), jnp.float32),
        ],
        scratch_shapes=[pltpu.VMEM((BLOCKS, rows, rows), jnp.float32)] * 2
        + [pltpu.VMEM((TILES_DEV, 16, TILE), jnp.float32)],
        name="query_pass",
    )(at, lists, queries, out_grad, keys, values, *pairs)


def key_pass(at, lists, keys, values, queries, out_grad, pairs, stats):
    rows, width = queries.shape
    return pl.pallas_call(
        key_kernel,
        in_specs=[SMEM] + [VMEM] * 14,
        out_specs=[VMEM] * 2,
        out_shape=[jax.ShapeDtypeStruct((rows, width), jnp.bfloat16)] * 2,
        scratch_shapes=[pltpu.VMEM((TILES_DEV, lists.shape[0], TILE), jnp.float32)],
        name="key_pass",
    )(at, lists, keys, values, queries, out_grad, *pairs, *stats)


def pack_kernel(slots_ref, counts_ref, k_ref, v_ref, q_ref, g_ref, kv_ref, qg_ref, lists_ref):
    kv_ref[0] = k_ref[...]
    kv_ref[1] = v_ref[...]
    qg_ref[0] = q_ref[...]
    qg_ref[1] = g_ref[...]
    slots, tiles = slots_ref.shape
    side = 128
    for first in range(0, tiles, side):
        width = min(side, tiles - first)
        block = slots_ref[:, first : first + width]
        used = lax.broadcasted_iota(jnp.int32, block.shape, 0) < counts_ref[:, first : first + width]
        block = jnp.where(used, block, DEAD)
        block = jnp.concatenate([block, jnp.full((16 - slots, width), DEAD, jnp.int32)], axis=0)
        if width < side:
            block = jnp.concatenate([block, jnp.full((16, side - width), DEAD, jnp.int32)], axis=1)
        block = jnp.concatenate([block, jnp.full((side - 16, side), DEAD, jnp.int32)], axis=0)
        lists_ref[first : first + width] = block.T[:width]


def pack(slots, counts, keys, values, queries, out_grad):
    pair = jax.ShapeDtypeStruct((2,) + keys.shape, keys.dtype)
    return pl.pallas_call(
        pack_kernel,
        in_specs=[VMEM] * 6,
        out_specs=[VMEM] * 3,
        out_shape=[pair, pair, jax.ShapeDtypeStruct((slots.shape[1], 128), jnp.int32)],
        name="pack",
    )(slots, counts, keys, values, queries, out_grad)


def start_input(at_ref, pieces, w_ref, sems):
    rows = pieces[0].shape[1]
    copies = []
    for j in range(2):
        for i, piece in enumerate(pieces):
            place = (at_ref[0] % 4) ^ (i % 4)
            copy = pltpu.make_async_copy(
                piece.at[j],
                w_ref.at[j, i // 4, pl.ds(pl.multiple_of(place * rows, 64), rows)],
                sems.at[8 * j + i],
            )
            copy.start()
            copies.append(copy)
    return copies


def finish_input(at_ref, q_ref, x_ref, copies, w_ref, o_ref, out_ref, sems):
    span = w_ref.shape[2]
    own = q_ref[...]
    other = x_ref[...]
    outs = []
    for j in range(2):
        for copy in copies[8 * j : 8 * j + 8]:
            copy.wait()
        part = nt(own, w_ref[j, 0]) + nt(other, w_ref[j, 1])
        o_ref[j] = part.astype(o_ref.dtype)
        first = pl.multiple_of((at_ref[0] % 8 // 4 ^ j) * span, span)
        copy = pltpu.make_async_copy(o_ref.at[j], out_ref.at[:, pl.ds(first, span)], sems.at[j])
        copy.start()
        outs.append(copy)
    for copy in outs:
        copy.wait()


def final_kernel(*refs):
    at_ref = refs[0]
    key_args, refs = refs[:15], refs[15:]
    own_ref, other_ref = refs[:2]
    pieces, refs = refs[2:10], refs[10:]
    dk_ref, dv_ref, out_ref, mask_ref, w_ref, o_ref, sems, out_sems = refs
    copies = start_input(at_ref, pieces, w_ref, sems)
    key_kernel(*key_args, dk_ref, dv_ref, mask_ref)
    finish_input(at_ref, own_ref, other_ref, copies, w_ref, o_ref, out_ref, out_sems)


def final_pass(at, lists, keys, values, queries, out_grad, pairs, stats, own, other, pieces):
    rows, width = queries.shape
    span = pieces[0].shape[1] * 4
    return pl.pallas_call(
        final_kernel,
        in_specs=[SMEM] + [VMEM] * 16 + [ANYWHERE] * 8,
        out_specs=[VMEM, VMEM, ANYWHERE],
        out_shape=[jax.ShapeDtypeStruct((rows, width), jnp.bfloat16)] * 2
        + [jax.ShapeDtypeStruct((rows, 2 * span), jnp.bfloat16)],
        scratch_shapes=[
            pltpu.VMEM((TILES_DEV, lists.shape[0], TILE), jnp.float32),
            pltpu.VMEM((2, 2, span, width), jnp.bfloat16),
            pltpu.VMEM((2, rows, span), jnp.bfloat16),
            pltpu.SemaphoreType.DMA((16,)),
            pltpu.SemaphoreType.DMA((2,)),
        ],
        name="final_pass",
    )(at, lists, keys, values, queries, out_grad, *pairs, *stats, own, other, *pieces)


def spread_weight(weight, position, group):
    by_one = move(weight, lambda i: i ^ 4)
    by_two = move(weight, lambda i: i ^ 8)
    middle = move(weight, lambda i: i ^ 12 if 4 <= i < 12 else -1)
    outer = move(by_two, lambda i: i ^ 4 if 4 <= i < 12 else -1)
    by_three = jnp.where((position >= 4) & (position < 12), middle, outer)
    near = jnp.stack([weight, by_one])
    away = jnp.stack([by_two, by_three])
    same = position // 8 == group
    kept = jnp.where(same, near, away)
    sent = jnp.where(same, away, near)
    swapped = swap_groups(sent)
    pieces = []
    for held in (kept, swapped):
        paired = move(held, to_frame_pair)
        core = move(held, to_core)
        pieces += [held, core, paired, move(paired, to_core)]
    return pieces


def input_by_gather(query_grad, weight):
    size, groups = lax.axis_size("seq"), lax.axis_size("head")
    part = size // groups
    route = []
    for p in range(size):
        for c in range(groups):
            high, low = divmod(p, part)
            route.append((p * groups + c, (c * part + low) * groups + high))
    regrouped = lax.ppermute(weight, ("seq", "head"), route)
    gathered = lax.all_gather(regrouped, "seq", axis=0, tiled=True)
    gathered = gathered.reshape(groups, -1, weight.shape[1])
    rows = lax.all_gather(query_grad, "head")
    total = jnp.einsum("grk,gck->rc", rows, gathered, preferred_element_type=jnp.float32)
    return total.astype(jnp.bfloat16)


def gradients(
    queries, key_rows, value_rows, out_grad, query_weight, neighbour_tiles, neighbour_count
):
    position = lax.axis_index("seq")
    direct = lax.axis_size("seq") == 16 and lax.axis_size("head") == 2
    kv_pair, qg_pair, lists = pack(
        neighbour_tiles.T, neighbour_count[None], key_rows, value_rows, queries, out_grad
    )
    if direct:
        pieces = spread_weight(query_weight, position, lax.axis_index("head"))
    at = jnp.full((1,), position, jnp.int32)

    def window(pair):
        near = move(pair, to_frame_pair)
        far = move(near, to_next_pair)
        core = move(pair, to_core)
        near_core = move(near, to_core)
        return [core, near, near_core, far, move(far, to_core)]

    kv_pairs = window(kv_pair)
    qg_pairs = window(qg_pair)
    query_grad, own = query_pass(
        at, lists, queries, out_grad, key_rows, value_rows, kv_pairs
    )
    core = move(own, to_core)
    both = jnp.concatenate([own, core])
    stats = [own, core, move(both, to_frame_pair), move(both, to_far_pair)]
    if direct:
        swapped = swap_groups(query_grad)
        key_grad, value_grad, input_grad = final_pass(
            at, lists, key_rows, value_rows, queries, out_grad, qg_pairs, stats,
            query_grad, swapped, pieces,
        )
    else:
        input_grad = input_by_gather(query_grad, query_weight)
        key_grad, value_grad = key_pass(
            at, lists, key_rows, value_rows, queries, out_grad, qg_pairs, stats
        )
    return (input_grad, key_grad, value_grad)


def solution(mesh):
    placed = (
        P("seq", "head"),
        P("seq", "head"),
        P("seq", "head"),
        P("seq", "head"),
        P("seq", "head"),
        P(),
        P(),
    )
    return jax.shard_map(
        gradients,
        mesh=mesh,
        in_specs=placed,
        out_specs=(P("seq", "head"), P("seq", "head"), P("seq", "head")),
        check_vma=False,
    )
```

```python
import jax
import jax.numpy as jnp
from jax import lax
from jax.experimental import pallas as pl
from jax.experimental.pallas import tpu as pltpu
from jax.sharding import PartitionSpec as P

HEAD_DIM = 128
HEADS_DEV = 3
TILE = 128
TILES_DEV = 2
SCALE = HEAD_DIM ** (-0.5)
LOG2_E = 1.4426950408889634
SCALE_2 = SCALE * LOG2_E
BLOCKS = 6
DEAD = -64


def move(block, route):
    size = lax.axis_size("seq")
    pairs = [(i, route(i)) for i in range(size)]
    return lax.ppermute(block, "seq", [(i, j) for i, j in pairs if 0 <= j < size])


def swap_groups(block):
    return lax.ppermute(block, "head", [(0, 1), (1, 0)])


def to_core(i):
    return i ^ 1


def to_frame_pair(i):
    return i ^ 2


def to_next_pair(i):
    return i + 4 if i % 4 < 2 else i - 4


def to_far_pair(i):
    return i - 2 if i % 4 < 2 else i + 2


def owners(position):
    far = jnp.where(position % 4 < 2, position - 2, position + 2)
    return [position, position ^ 1, position ^ 2, position ^ 3, far, far ^ 1]


def nt(left, right):
    return lax.dot_general(
        left, right, (((1,), (1,)), ((), ())), preferred_element_type=jnp.float32
    )


def tn(left, right):
    return lax.dot_general(
        left, right, (((0,), (0,)), ((), ())), preferred_element_type=jnp.float32
    )


def any_lane(hits):
    best = jnp.max(jnp.where(hits, 1.0, 0.0), axis=1, keepdims=True)
    return jnp.where(best > 0.0, 0.0, -jnp.inf)


def own_query_masks(position, lists_ref, mask_ref):
    row = lax.broadcasted_iota(jnp.int32, (16, lists_ref.shape[1]), 0)
    tile = jnp.full(row.shape, 2 * DEAD, jnp.int32)
    for b, owner in enumerate(owners(position)):
        tile = jnp.where(row // TILES_DEV == b, owner * TILES_DEV + row % TILES_DEV, tile)
    for c in range(TILES_DEV):
        own = lists_ref[pl.ds(position * TILES_DEV + c, 1)]
        mask_ref[c] = jnp.broadcast_to(any_lane(own == tile), mask_ref.shape[1:])


def own_key_masks(position, lists_ref, mask_ref):
    for a in range(TILES_DEV):
        hits = lists_ref[...] == position * TILES_DEV + a
        mask_ref[a] = jnp.broadcast_to(any_lane(hits), mask_ref.shape[1:])


def query_kernel(
    at_ref, lists_ref, q_ref, g_ref, k_ref, v_ref, b1, b2, b3, b4, b5,
    dq_ref, stat_ref, s_ref, d_ref, mask_ref,
):
    own_query_masks(at_ref[0], lists_ref, mask_ref)
    stat_ref[...] = jnp.zeros_like(stat_ref)
    half = q_ref.shape[0] // TILES_DEV
    pairs = [b1, b2, b3, b4, b5]

    def mask(b, a):
        at = TILES_DEV * b + a
        return jnp.concatenate([mask_ref[0, at : at + 1], mask_ref[1, at : at + 1]], axis=1)

    def columns(head):
        return slice(head * HEAD_DIM, (head + 1) * HEAD_DIM)

    def key(head, b):
        return k_ref[:, columns(head)] if b == 0 else pairs[b - 1][0, :, columns(head)]

    def value(head, b):
        return v_ref[:, columns(head)] if b == 0 else pairs[b - 1][1, :, columns(head)]

    top = [None] * HEADS_DEV
    total = [0.0] * HEADS_DEV
    delta = [0.0] * HEADS_DEV
    acc = [0.0] * HEADS_DEV

    def products(head, b):
        scores = nt(key(head, b), q_ref[:, columns(head)])
        s_ref[head, b] = scores
        d_ref[head, b] = nt(value(head, b), g_ref[:, columns(head)])
        for a in range(TILES_DEV):
            peak = jnp.max(scores[a * half : (a + 1) * half], axis=0, keepdims=True)
            peak = peak * SCALE_2 + mask(b, a)
            top[head] = peak if top[head] is None else jnp.maximum(top[head], peak)

    def weigh(head, b):
        for a in range(TILES_DEV):
            part = slice(a * half, (a + 1) * half)
            weight = jnp.exp2(s_ref[head, b, part] * SCALE_2 - (top[head] - mask(b, a)))
            s_ref[head, b, part] = weight
            dprobs = d_ref[head, b, part]
            total[head] = total[head] + jnp.sum(weight, axis=0, keepdims=True)
            delta[head] = delta[head] + jnp.sum(weight * dprobs, axis=0, keepdims=True)

    def gather(head, b):
        dscores = (s_ref[head, b] * (d_ref[head, b] - delta[head])).astype(jnp.bfloat16)
        acc[head] = acc[head] + tn(key(head, b), dscores)

    for step in range(HEADS_DEV + 2):
        for b in range(BLOCKS):
            if step < HEADS_DEV:
                products(step, b)
            if 0 <= step - 1 < HEADS_DEV:
                weigh(step - 1, b)
            if 0 <= step - 2:
                gather(step - 2, b)
        if 0 <= step - 1 < HEADS_DEV:
            head = step - 1
            delta[head] = delta[head] / total[head]
            stat_ref[head : head + 1] = top[head] + jnp.log(total[head]) * LOG2_E
            stat_ref[head + HEADS_DEV : head + HEADS_DEV + 1] = delta[head]
        if 0 <= step - 2:
            head = step - 2
            scaled = acc[head] * (SCALE / total[head])
            dq_ref[:, columns(head)] = scaled.T.astype(jnp.bfloat16)


def key_kernel(
    at_ref, lists_ref, k_ref, v_ref, q_ref, g_ref, b1, b2, b3, b4, b5,
    t0, t1, t2, t4, dk_ref, dv_ref, mask_ref,
):
    tiles = lists_ref.shape[0]
    own_key_masks(at_ref[0], lists_ref, mask_ref)
    half = k_ref.shape[0] // TILES_DEV
    pairs = [b1, b2, b3, b4, b5]
    stats = [(t0, 0), (t1, 0), (t2, 0), (t2, 8), (t4, 0), (t4, 8)]
    masks = []
    for owner in owners(at_ref[0]):
        first = owner * TILES_DEV
        inside = (first >= 0) & (first < tiles)
        there = jnp.where(inside, 0.0, -jnp.inf)
        row = jnp.where(inside, first, 0)
        masks.append([
            jnp.concatenate([mask_ref[a, pl.ds(row + c, 1)] for c in range(TILES_DEV)], axis=1)
            + there
            for a in range(TILES_DEV)
        ])

    def operands(head, b):
        cols = slice(head * HEAD_DIM, (head + 1) * HEAD_DIM)
        if b == 0:
            return q_ref[:, cols], g_ref[:, cols]
        return pairs[b - 1][0, :, cols], pairs[b - 1][1, :, cols]

    def products(head, b):
        cols = slice(head * HEAD_DIM, (head + 1) * HEAD_DIM)
        query, grad = operands(head, b)
        return nt(k_ref[:, cols], query), nt(v_ref[:, cols], grad)

    def soften(head, b, scores, dprobs):
        stat, at = stats[b]
        log_norm = stat[at + head : at + head + 1]
        at += HEADS_DEV
        delta = stat[at + head : at + head + 1]
        low, dscores = [], []
        for a in range(TILES_DEV):
            part = slice(a * half, (a + 1) * half)
            probs = jnp.exp2(scores[part] * SCALE_2 - (log_norm - masks[b][a]))
            low.append(probs.astype(jnp.bfloat16))
            dscores.append((probs * (dprobs[part] - delta)).astype(jnp.bfloat16))
        return jnp.concatenate(low, axis=0), jnp.concatenate(dscores, axis=0)

    work = [(head, b) for head in range(HEADS_DEV) for b in range(BLOCKS)]
    ahead = {}
    soft = {}
    for i in range(len(work) + 2):
        if i < len(work):
            ahead[i] = products(*work[i])
        if 1 <= i <= len(work):
            soft[i - 1] = soften(*work[i - 1], *ahead.pop(i - 1))
        if i < 2:
            continue
        head, b = work[i - 2]
        low, dscores = soft.pop(i - 2)
        query, grad = operands(head, b)
        value_term = jnp.dot(low, grad, preferred_element_type=jnp.float32)
        key_term = jnp.dot(dscores, query, preferred_element_type=jnp.float32)
        value_acc = value_term if b == 0 else value_acc + value_term
        key_acc = key_term if b == 0 else key_acc + key_term
        if b == BLOCKS - 1:
            cols = slice(head * HEAD_DIM, (head + 1) * HEAD_DIM)
            dk_ref[:, cols] = (key_acc * SCALE).astype(jnp.bfloat16)
            dv_ref[:, cols] = value_acc.astype(jnp.bfloat16)


SMEM = pl.BlockSpec(memory_space=pltpu.SMEM)
VMEM = pl.BlockSpec(memory_space=pltpu.VMEM)
ANYWHERE = pl.BlockSpec(memory_space=pl.ANY)


def query_pass(at, lists, queries, out_grad, keys, values, pairs):
    rows, width = queries.shape
    return pl.pallas_call(
        query_kernel,
        in_specs=[SMEM] + [VMEM] * 10,
        out_specs=[VMEM] * 2,
        out_shape=[
            jax.ShapeDtypeStruct((rows, width), jnp.bfloat16),
            jax.ShapeDtypeStruct((8, rows), jnp.float32),
        ],
        scratch_shapes=[pltpu.VMEM((HEADS_DEV, BLOCKS, rows, rows), jnp.float32)] * 2
        + [pltpu.VMEM((TILES_DEV, 16, TILE), jnp.float32)],
        compiler_params=pltpu.CompilerParams(vmem_limit_bytes=24 * 2**20),
        name="query_pass",
    )(at, lists, queries, out_grad, keys, values, *pairs)


def key_pass(at, lists, keys, values, queries, out_grad, pairs, stats):
    rows, width = queries.shape
    return pl.pallas_call(
        key_kernel,
        in_specs=[SMEM] + [VMEM] * 14,
        out_specs=[VMEM] * 2,
        out_shape=[jax.ShapeDtypeStruct((rows, width), jnp.bfloat16)] * 2,
        scratch_shapes=[pltpu.VMEM((TILES_DEV, lists.shape[0], TILE), jnp.float32)],
        name="key_pass",
    )(at, lists, keys, values, queries, out_grad, *pairs, *stats)


def pack_kernel(slots_ref, counts_ref, k_ref, v_ref, q_ref, g_ref, kv_ref, qg_ref, lists_ref):
    kv_ref[0] = k_ref[...]
    kv_ref[1] = v_ref[...]
    qg_ref[0] = q_ref[...]
    qg_ref[1] = g_ref[...]
    slots, tiles = slots_ref.shape
    side = 128
    for first in range(0, tiles, side):
        width = min(side, tiles - first)
        block = slots_ref[:, first : first + width]
        used = lax.broadcasted_iota(jnp.int32, block.shape, 0) < counts_ref[:, first : first + width]
        block = jnp.where(used, block, DEAD)
        block = jnp.concatenate([block, jnp.full((16 - slots, width), DEAD, jnp.int32)], axis=0)
        if width < side:
            block = jnp.concatenate([block, jnp.full((16, side - width), DEAD, jnp.int32)], axis=1)
        block = jnp.concatenate([block, jnp.full((side - 16, side), DEAD, jnp.int32)], axis=0)
        lists_ref[first : first + width] = block.T[:width]


def pack(slots, counts, keys, values, queries, out_grad):
    pair = jax.ShapeDtypeStruct((2,) + keys.shape, keys.dtype)
    return pl.pallas_call(
        pack_kernel,
        in_specs=[VMEM] * 6,
        out_specs=[VMEM] * 3,
        out_shape=[pair, pair, jax.ShapeDtypeStruct((slots.shape[1], 128), jnp.int32)],
        name="pack",
    )(slots, counts, keys, values, queries, out_grad)


def place_pieces(at_ref, pieces, w_ref):
    rows = pieces[0].shape[1]
    for j in range(2):
        for i, piece in enumerate(pieces):
            place = (at_ref[0] % 4) ^ (i % 4)
            w_ref[j, i // 4, pl.ds(pl.multiple_of(place * rows, 64), rows)] = piece[j]


def input_product(at_ref, q_ref, x_ref, w_ref, o_ref, out_ref, sems):
    span = w_ref.shape[2]
    own = q_ref[...]
    other = x_ref[...]
    outs = []
    for j in range(2):
        part = nt(own, w_ref[j, 0]) + nt(other, w_ref[j, 1])
        o_ref[j] = part.astype(o_ref.dtype)
        first = pl.multiple_of((at_ref[0] % 8 // 4 ^ j) * span, span)
        copy = pltpu.make_async_copy(o_ref.at[j], out_ref.at[:, pl.ds(first, span)], sems.at[j])
        copy.start()
        outs.append(copy)
    for copy in outs:
        copy.wait()


def final_kernel(*refs):
    at_ref = refs[0]
    key_args, refs = refs[:15], refs[15:]
    own_ref, other_ref = refs[:2]
    pieces, refs = refs[2:10], refs[10:]
    dk_ref, dv_ref, out_ref, mask_ref, w_ref, o_ref, sems = refs
    place_pieces(at_ref, pieces, w_ref)
    key_kernel(*key_args, dk_ref, dv_ref, mask_ref)
    input_product(at_ref, own_ref, other_ref, w_ref, o_ref, out_ref, sems)


def final_pass(at, lists, keys, values, queries, out_grad, pairs, stats, own, other, pieces):
    rows, width = queries.shape
    span = pieces[0].shape[1] * 4
    return pl.pallas_call(
        final_kernel,
        in_specs=[SMEM] + [VMEM] * 24,
        out_specs=[VMEM, VMEM, ANYWHERE],
        out_shape=[jax.ShapeDtypeStruct((rows, width), jnp.bfloat16)] * 2
        + [jax.ShapeDtypeStruct((rows, 2 * span), jnp.bfloat16)],
        scratch_shapes=[
            pltpu.VMEM((TILES_DEV, lists.shape[0], TILE), jnp.float32),
            pltpu.VMEM((2, 2, span, width), jnp.bfloat16),
            pltpu.VMEM((2, rows, span), jnp.bfloat16),
            pltpu.SemaphoreType.DMA((2,)),
        ],
        compiler_params=pltpu.CompilerParams(vmem_limit_bytes=24 * 2**20),
        name="final_pass",
    )(at, lists, keys, values, queries, out_grad, *pairs, *stats, own, other, *pieces)


def spread_weight(weight, position, group):
    by_one = move(weight, lambda i: i ^ 4)
    by_two = move(weight, lambda i: i ^ 8)
    middle = move(weight, lambda i: i ^ 12 if 4 <= i < 12 else -1)
    outer = move(by_two, lambda i: i ^ 4 if 4 <= i < 12 else -1)
    by_three = jnp.where((position >= 4) & (position < 12), middle, outer)
    near = jnp.stack([weight, by_one])
    away = jnp.stack([by_two, by_three])
    same = position // 8 == group
    kept = jnp.where(same, near, away)
    sent = jnp.where(same, away, near)
    swapped = swap_groups(sent)
    pieces = []
    for held in (kept, swapped):
        paired = move(held, to_frame_pair)
        core = move(held, to_core)
        pieces += [held, core, paired, move(paired, to_core)]
    return pieces


def input_by_gather(query_grad, weight):
    size, groups = lax.axis_size("seq"), lax.axis_size("head")
    part = size // groups
    route = []
    for p in range(size):
        for c in range(groups):
            high, low = divmod(p, part)
            route.append((p * groups + c, (c * part + low) * groups + high))
    regrouped = lax.ppermute(weight, ("seq", "head"), route)
    gathered = lax.all_gather(regrouped, "seq", axis=0, tiled=True)
    gathered = gathered.reshape(groups, -1, weight.shape[1])
    rows = lax.all_gather(query_grad, "head")
    total = jnp.einsum("grk,gck->rc", rows, gathered, preferred_element_type=jnp.float32)
    return total.astype(jnp.bfloat16)


def gradients(
    queries, key_rows, value_rows, out_grad, query_weight, neighbour_tiles, neighbour_count
):
    position = lax.axis_index("seq")
    direct = lax.axis_size("seq") == 16 and lax.axis_size("head") == 2
    kv_pair, qg_pair, lists = pack(
        neighbour_tiles.T, neighbour_count[None], key_rows, value_rows, queries, out_grad
    )
    if direct:
        pieces = spread_weight(query_weight, position, lax.axis_index("head"))
    at = jnp.full((1,), position, jnp.int32)

    def window(pair):
        near = move(pair, to_frame_pair)
        far = move(near, to_next_pair)
        core = move(pair, to_core)
        near_core = move(near, to_core)
        return [core, near, near_core, far, move(far, to_core)]

    kv_pairs = window(kv_pair)
    qg_pairs = window(qg_pair)
    query_grad, own = query_pass(
        at, lists, queries, out_grad, key_rows, value_rows, kv_pairs
    )
    core = move(own, to_core)
    both = jnp.concatenate([own, core])
    stats = [own, core, move(both, to_frame_pair), move(both, to_far_pair)]
    if direct:
        swapped = swap_groups(query_grad)
        key_grad, value_grad, input_grad = final_pass(
            at, lists, key_rows, value_rows, queries, out_grad, qg_pairs, stats,
            query_grad, swapped, pieces,
        )
    else:
        input_grad = input_by_gather(query_grad, query_weight)
        key_grad, value_grad = key_pass(
            at, lists, key_rows, value_rows, queries, out_grad, qg_pairs, stats
        )
    return (input_grad, key_grad, value_grad)


def solution(mesh):
    placed = (
        P("seq", "head"),
        P("seq", "head"),
        P("seq", "head"),
        P("seq", "head"),
        P("seq", "head"),
        P(),
        P(),
    )
    return jax.shard_map(
        gradients,
        mesh=mesh,
        in_specs=placed,
        out_specs=(P("seq", "head"), P("seq", "head"), P("seq", "head")),
        check_vma=False,
    )
```

```python
import jax
import jax.numpy as jnp
from jax import lax
from jax.experimental import pallas as pl
from jax.experimental.pallas import tpu as pltpu
from jax.sharding import PartitionSpec as P

HEAD_DIM = 128
HEADS_DEV = 3
TILE = 128
TILES_DEV = 2
SCALE = HEAD_DIM ** (-0.5)
LOG2_E = 1.4426950408889634
SCALE_2 = SCALE * LOG2_E
BLOCKS = 6
DEAD = -64


def move(block, route):
    size = lax.axis_size("seq")
    pairs = [(i, route(i)) for i in range(size)]
    return lax.ppermute(block, "seq", [(i, j) for i, j in pairs if 0 <= j < size])


def swap_groups(block):
    return lax.ppermute(block, "head", [(0, 1), (1, 0)])


def to_core(i):
    return i ^ 1


def to_frame_pair(i):
    return i ^ 2


def to_next_pair(i):
    return i + 4 if i % 4 < 2 else i - 4


def to_far_pair(i):
    return i - 2 if i % 4 < 2 else i + 2


def owners(position):
    far = jnp.where(position % 4 < 2, position - 2, position + 2)
    return [position, position ^ 1, position ^ 2, position ^ 3, far, far ^ 1]


def nt(left, right):
    return lax.dot_general(
        left, right, (((1,), (1,)), ((), ())), preferred_element_type=jnp.float32
    )


def tn(left, right):
    return lax.dot_general(
        left, right, (((0,), (0,)), ((), ())), preferred_element_type=jnp.float32
    )


def any_lane(hits):
    best = jnp.max(jnp.where(hits, 1.0, 0.0), axis=1, keepdims=True)
    return jnp.where(best > 0.0, 0.0, -jnp.inf)


def own_query_masks(position, lists_ref, mask_ref):
    row = lax.broadcasted_iota(jnp.int32, (16, lists_ref.shape[1]), 0)
    tile = jnp.full(row.shape, 2 * DEAD, jnp.int32)
    for b, owner in enumerate(owners(position)):
        tile = jnp.where(row // TILES_DEV == b, owner * TILES_DEV + row % TILES_DEV, tile)
    for c in range(TILES_DEV):
        own = lists_ref[pl.ds(position * TILES_DEV + c, 1)]
        mask_ref[c] = jnp.broadcast_to(any_lane(own == tile), mask_ref.shape[1:])


def own_key_masks(position, lists_ref, mask_ref):
    for a in range(TILES_DEV):
        hits = lists_ref[...] == position * TILES_DEV + a
        mask_ref[a] = jnp.broadcast_to(any_lane(hits), mask_ref.shape[1:])


def query_kernel(
    at_ref, lists_ref, q_ref, g_ref, k_ref, v_ref, b1, b2, b3, b4, b5,
    dq_ref, stat_ref, s_ref, d_ref, mask_ref,
):
    own_query_masks(at_ref[0], lists_ref, mask_ref)
    stat_ref[...] = jnp.zeros_like(stat_ref)
    half = q_ref.shape[0] // TILES_DEV
    pairs = [b1, b2, b3, b4, b5]

    def mask(b, a):
        at = TILES_DEV * b + a
        return jnp.concatenate([mask_ref[0, at : at + 1], mask_ref[1, at : at + 1]], axis=1)

    def columns(head):
        return slice(head * HEAD_DIM, (head + 1) * HEAD_DIM)

    def key(head, b):
        return k_ref[:, columns(head)] if b == 0 else pairs[b - 1][0, :, columns(head)]

    def value(head, b):
        return v_ref[:, columns(head)] if b == 0 else pairs[b - 1][1, :, columns(head)]

    top = [None] * HEADS_DEV
    total = [0.0] * HEADS_DEV
    delta = [0.0] * HEADS_DEV
    acc = [0.0] * HEADS_DEV

    def products(head, b):
        scores = nt(key(head, b), q_ref[:, columns(head)])
        s_ref[head, b] = scores
        d_ref[head, b] = nt(value(head, b), g_ref[:, columns(head)])
        for a in range(TILES_DEV):
            peak = jnp.max(scores[a * half : (a + 1) * half], axis=0, keepdims=True)
            peak = peak * SCALE_2 + mask(b, a)
            top[head] = peak if top[head] is None else jnp.maximum(top[head], peak)

    def weigh(head, b):
        for a in range(TILES_DEV):
            part = slice(a * half, (a + 1) * half)
            weight = jnp.exp2(s_ref[head, b, part] * SCALE_2 - (top[head] - mask(b, a)))
            s_ref[head, b, part] = weight
            dprobs = d_ref[head, b, part]
            total[head] = total[head] + jnp.sum(weight, axis=0, keepdims=True)
            delta[head] = delta[head] + jnp.sum(weight * dprobs, axis=0, keepdims=True)

    def gather(head, b):
        dscores = (s_ref[head, b] * (d_ref[head, b] - delta[head])).astype(jnp.bfloat16)
        acc[head] = acc[head] + tn(key(head, b), dscores)

    for step in range(HEADS_DEV + 2):
        for b in range(BLOCKS):
            if step < HEADS_DEV:
                products(step, b)
            if 0 <= step - 1 < HEADS_DEV:
                weigh(step - 1, b)
            if 0 <= step - 2:
                gather(step - 2, b)
        if 0 <= step - 1 < HEADS_DEV:
            head = step - 1
            delta[head] = delta[head] / total[head]
            stat_ref[head : head + 1] = top[head] + jnp.log(total[head]) * LOG2_E
            stat_ref[head + HEADS_DEV : head + HEADS_DEV + 1] = delta[head]
        if 0 <= step - 2:
            head = step - 2
            scaled = acc[head] * (SCALE / total[head])
            dq_ref[:, columns(head)] = scaled.T.astype(jnp.bfloat16)


def key_kernel(
    at_ref, lists_ref, k_ref, v_ref, q_ref, g_ref, b1, b2, b3, b4, b5,
    t0, t1, t2, t4, dk_ref, dv_ref, mask_ref,
):
    tiles = lists_ref.shape[0]
    own_key_masks(at_ref[0], lists_ref, mask_ref)
    half = k_ref.shape[0] // TILES_DEV
    pairs = [b1, b2, b3, b4, b5]
    stats = [(t0, 0), (t1, 0), (t2, 0), (t2, 8), (t4, 0), (t4, 8)]
    masks = []
    for owner in owners(at_ref[0]):
        first = owner * TILES_DEV
        inside = (first >= 0) & (first < tiles)
        there = jnp.where(inside, 0.0, -jnp.inf)
        row = jnp.where(inside, first, 0)
        masks.append([
            jnp.concatenate([mask_ref[a, pl.ds(row + c, 1)] for c in range(TILES_DEV)], axis=1)
            + there
            for a in range(TILES_DEV)
        ])

    def operands(head, b):
        cols = slice(head * HEAD_DIM, (head + 1) * HEAD_DIM)
        if b == 0:
            return q_ref[:, cols], g_ref[:, cols]
        return pairs[b - 1][0, :, cols], pairs[b - 1][1, :, cols]

    def products(head, b):
        cols = slice(head * HEAD_DIM, (head + 1) * HEAD_DIM)
        query, grad = operands(head, b)
        return nt(k_ref[:, cols], query), nt(v_ref[:, cols], grad)

    def soften(head, b, scores, dprobs):
        stat, at = stats[b]
        log_norm = stat[at + head : at + head + 1]
        at += HEADS_DEV
        delta = stat[at + head : at + head + 1]
        low, dscores = [], []
        for a in range(TILES_DEV):
            part = slice(a * half, (a + 1) * half)
            probs = jnp.exp2(scores[part] * SCALE_2 - (log_norm - masks[b][a]))
            low.append(probs.astype(jnp.bfloat16))
            dscores.append((probs * (dprobs[part] - delta)).astype(jnp.bfloat16))
        return jnp.concatenate(low, axis=0), jnp.concatenate(dscores, axis=0)

    work = [(head, b) for head in range(HEADS_DEV) for b in range(BLOCKS)]
    ahead = {}
    soft = {}
    for i in range(len(work) + 2):
        if i < len(work):
            ahead[i] = products(*work[i])
        if 1 <= i <= len(work):
            soft[i - 1] = soften(*work[i - 1], *ahead.pop(i - 1))
        if i < 2:
            continue
        head, b = work[i - 2]
        low, dscores = soft.pop(i - 2)
        query, grad = operands(head, b)
        value_term = jnp.dot(low, grad, preferred_element_type=jnp.float32)
        key_term = jnp.dot(dscores, query, preferred_element_type=jnp.float32)
        value_acc = value_term if b == 0 else value_acc + value_term
        key_acc = key_term if b == 0 else key_acc + key_term
        if b == BLOCKS - 1:
            cols = slice(head * HEAD_DIM, (head + 1) * HEAD_DIM)
            dk_ref[:, cols] = (key_acc * SCALE).astype(jnp.bfloat16)
            dv_ref[:, cols] = value_acc.astype(jnp.bfloat16)


SMEM = pl.BlockSpec(memory_space=pltpu.SMEM)
VMEM = pl.BlockSpec(memory_space=pltpu.VMEM)
ANYWHERE = pl.BlockSpec(memory_space=pl.ANY)


def query_pass(at, lists, queries, out_grad, keys, values, pairs):
    rows, width = queries.shape
    return pl.pallas_call(
        query_kernel,
        in_specs=[SMEM] + [VMEM] * 10,
        out_specs=[VMEM] * 2,
        out_shape=[
            jax.ShapeDtypeStruct((rows, width), jnp.bfloat16),
            jax.ShapeDtypeStruct((8, rows), jnp.float32),
        ],
        scratch_shapes=[pltpu.VMEM((HEADS_DEV, BLOCKS, rows, rows), jnp.float32)] * 2
        + [pltpu.VMEM((TILES_DEV, 16, TILE), jnp.float32)],
        compiler_params=pltpu.CompilerParams(vmem_limit_bytes=24 * 2**20),
        name="query_pass",
    )(at, lists, queries, out_grad, keys, values, *pairs)


def key_pass(at, lists, keys, values, queries, out_grad, pairs, stats):
    rows, width = queries.shape
    return pl.pallas_call(
        key_kernel,
        in_specs=[SMEM] + [VMEM] * 14,
        out_specs=[VMEM] * 2,
        out_shape=[jax.ShapeDtypeStruct((rows, width), jnp.bfloat16)] * 2,
        scratch_shapes=[pltpu.VMEM((TILES_DEV, lists.shape[0], TILE), jnp.float32)],
        name="key_pass",
    )(at, lists, keys, values, queries, out_grad, *pairs, *stats)


def pack_kernel(slots_ref, counts_ref, k_ref, v_ref, q_ref, g_ref, kv_ref, qg_ref, lists_ref):
    kv_ref[0] = k_ref[...]
    kv_ref[1] = v_ref[...]
    qg_ref[0] = q_ref[...]
    qg_ref[1] = g_ref[...]
    slots, tiles = slots_ref.shape
    side = 128
    for first in range(0, tiles, side):
        width = min(side, tiles - first)
        block = slots_ref[:, first : first + width]
        used = lax.broadcasted_iota(jnp.int32, block.shape, 0) < counts_ref[:, first : first + width]
        block = jnp.where(used, block, DEAD)
        block = jnp.concatenate([block, jnp.full((16 - slots, width), DEAD, jnp.int32)], axis=0)
        if width < side:
            block = jnp.concatenate([block, jnp.full((16, side - width), DEAD, jnp.int32)], axis=1)
        block = jnp.concatenate([block, jnp.full((side - 16, side), DEAD, jnp.int32)], axis=0)
        lists_ref[first : first + width] = block.T[:width]


def pack(slots, counts, keys, values, queries, out_grad):
    pair = jax.ShapeDtypeStruct((2,) + keys.shape, keys.dtype)
    return pl.pallas_call(
        pack_kernel,
        in_specs=[VMEM] * 6,
        out_specs=[VMEM] * 3,
        out_shape=[pair, pair, jax.ShapeDtypeStruct((slots.shape[1], 128), jnp.int32)],
        name="pack",
    )(slots, counts, keys, values, queries, out_grad)


def place_pieces(at_ref, pieces, w_ref):
    rows = pieces[0].shape[1]
    for j in range(2):
        for i in range(4):
            at = pl.ds(pl.multiple_of(((at_ref[0] % 4) ^ i) * rows, 64), rows)
            w_ref[j, 0, at] = pieces[i][j]
            w_ref[j, 1, at] = pieces[4 + 4 * j + i][...]


def input_product(at_ref, q_ref, x_ref, w_ref, o_ref, out_ref, sems):
    span = w_ref.shape[2]
    own = q_ref[...]
    other = x_ref[...]
    outs = []
    for j in range(2):
        part = nt(own, w_ref[j, 0]) + nt(other, w_ref[j, 1])
        o_ref[j] = part.astype(o_ref.dtype)
        first = pl.multiple_of((at_ref[0] % 8 // 4 ^ j) * span, span)
        copy = pltpu.make_async_copy(o_ref.at[j], out_ref.at[:, pl.ds(first, span)], sems.at[j])
        copy.start()
        outs.append(copy)
    for copy in outs:
        copy.wait()


def final_kernel(*refs):
    at_ref = refs[0]
    key_args, refs = refs[:15], refs[15:]
    own_ref, other_ref = refs[:2]
    pieces, refs = refs[2:14], refs[14:]
    dk_ref, dv_ref, out_ref, mask_ref, w_ref, o_ref, sems = refs
    place_pieces(at_ref, pieces, w_ref)
    key_kernel(*key_args, dk_ref, dv_ref, mask_ref)
    input_product(at_ref, own_ref, other_ref, w_ref, o_ref, out_ref, sems)


def final_pass(at, lists, keys, values, queries, out_grad, pairs, stats, own, other, pieces):
    rows, width = queries.shape
    span = pieces[0].shape[1] * 4
    return pl.pallas_call(
        final_kernel,
        in_specs=[SMEM] + [VMEM] * 28,
        out_specs=[VMEM, VMEM, ANYWHERE],
        out_shape=[jax.ShapeDtypeStruct((rows, width), jnp.bfloat16)] * 2
        + [jax.ShapeDtypeStruct((rows, 2 * span), jnp.bfloat16)],
        scratch_shapes=[
            pltpu.VMEM((TILES_DEV, lists.shape[0], TILE), jnp.float32),
            pltpu.VMEM((2, 2, span, width), jnp.bfloat16),
            pltpu.VMEM((2, rows, span), jnp.bfloat16),
            pltpu.SemaphoreType.DMA((2,)),
        ],
        compiler_params=pltpu.CompilerParams(vmem_limit_bytes=24 * 2**20),
        name="final_pass",
    )(at, lists, keys, values, queries, out_grad, *pairs, *stats, own, other, *pieces)


def spread_weight(weight, position, group):
    by_one = move(weight, lambda i: i ^ 4)
    by_two = move(weight, lambda i: i ^ 8)
    middle = move(weight, lambda i: i ^ 12 if 4 <= i < 12 else -1)
    outer = move(by_two, lambda i: i ^ 4 if 4 <= i < 12 else -1)
    by_three = jnp.where((position >= 4) & (position < 12), middle, outer)
    near = jnp.stack([weight, by_one])
    away = jnp.stack([by_two, by_three])
    same = position // 8 == group
    kept = jnp.where(same, near, away)
    paired = move(kept, to_frame_pair)
    pieces = [kept, move(kept, to_core), paired, move(paired, to_core)]
    for j in range(2):
        swapped = swap_groups(jnp.where(same, away[j], near[j]))
        paired = move(swapped, to_frame_pair)
        core = move(swapped, to_core)
        pieces += [swapped, core, paired, move(paired, to_core)]
    return pieces


def input_by_gather(query_grad, weight):
    size, groups = lax.axis_size("seq"), lax.axis_size("head")
    part = size // groups
    route = []
    for p in range(size):
        for c in range(groups):
            high, low = divmod(p, part)
            route.append((p * groups + c, (c * part + low) * groups + high))
    regrouped = lax.ppermute(weight, ("seq", "head"), route)
    gathered = lax.all_gather(regrouped, "seq", axis=0, tiled=True)
    gathered = gathered.reshape(groups, -1, weight.shape[1])
    rows = lax.all_gather(query_grad, "head")
    total = jnp.einsum("grk,gck->rc", rows, gathered, preferred_element_type=jnp.float32)
    return total.astype(jnp.bfloat16)


def gradients(
    queries, key_rows, value_rows, out_grad, query_weight, neighbour_tiles, neighbour_count
):
    position = lax.axis_index("seq")
    direct = lax.axis_size("seq") == 16 and lax.axis_size("head") == 2
    kv_pair, qg_pair, lists = pack(
        neighbour_tiles.T, neighbour_count[None], key_rows, value_rows, queries, out_grad
    )
    if direct:
        pieces = spread_weight(query_weight, position, lax.axis_index("head"))
    at = jnp.full((1,), position, jnp.int32)

    def window(pair):
        near = move(pair, to_frame_pair)
        far = move(near, to_next_pair)
        core = move(pair, to_core)
        near_core = move(near, to_core)
        return [core, near, near_core, far, move(far, to_core)]

    kv_pairs = window(kv_pair)
    qg_pairs = window(qg_pair)
    query_grad, own = query_pass(
        at, lists, queries, out_grad, key_rows, value_rows, kv_pairs
    )
    core = move(own, to_core)
    both = jnp.concatenate([own, core])
    stats = [own, core, move(both, to_frame_pair), move(both, to_far_pair)]
    if direct:
        swapped = swap_groups(query_grad)
        key_grad, value_grad, input_grad = final_pass(
            at, lists, key_rows, value_rows, queries, out_grad, qg_pairs, stats,
            query_grad, swapped, pieces,
        )
    else:
        input_grad = input_by_gather(query_grad, query_weight)
        key_grad, value_grad = key_pass(
            at, lists, key_rows, value_rows, queries, out_grad, qg_pairs, stats
        )
    return (input_grad, key_grad, value_grad)


def solution(mesh):
    placed = (
        P("seq", "head"),
        P("seq", "head"),
        P("seq", "head"),
        P("seq", "head"),
        P("seq", "head"),
        P(),
        P(),
    )
    return jax.shard_map(
        gradients,
        mesh=mesh,
        in_specs=placed,
        out_specs=(P("seq", "head"), P("seq", "head"), P("seq", "head")),
        check_vma=False,
    )
```
